32 devices in a mesh: shard: 8 (over z, core), rep: 4 (over y, x).
Axes of the slice: x: 2, y: 2, z: 4, core: 2. Of those that a mesh axis runs over, the one named last changes fastest.
Arguments:
- tokens: bfloat16 [49152, 640], P(('shard', 'rep')), may hold values from -6 to 6
- seq_lengths: int32 [64], replicated, may hold values from 256 to 1024, as said below
- seq_device: int32 [64], replicated, may hold values from 0 to 31, as said below
- w_query: bfloat16 [640, 1024], P('shard'), may hold values from -0.25 to 0.25
- w_keyval: bfloat16 [640, 512], P('shard'), may hold values from -0.25 to 0.25
- w_project: bfloat16 [1024, 640], P('shard'), may hold values from -0.1875 to 0.1875
- w_gate: bfloat16 [640, 2048], P('shard'), may hold values from -0.25 to 0.25
- w_upward: bfloat16 [640, 2048], P('shard'), may hold values from -0.25 to 0.25
- w_down: bfloat16 [2048, 640], P('shard'), may hold values from -0.125 to 0.125
- gain_input: bfloat16 [640], P('shard'), may hold values from 0.5 to 2
- gain_query: bfloat16 [256], P('shard'), may hold values from 0.5 to 2
- gain_key: bfloat16 [256], P('shard'), may hold values from 0.5 to 2
- gain_attend: bfloat16 [640], P('shard'), may hold values from 0.5 to 2
- gain_before: bfloat16 [640], P('shard'), may hold values from 0.5 to 2
- gain_after: bfloat16 [640], P('shard'), may hold values from 0.5 to 2
- cotangent: bfloat16 [49152, 640], P(('shard', 'rep')), may hold values from -6 to 6
Outputs:
- activations: bfloat16 [49152, 640], P(('shard', 'rep'))
- input_grad: float32 [49152, 640], P(('shard', 'rep'))
- query_grad: float32 [640, 1024], P('shard')
- keyval_grad: float32 [640, 512], P('shard')
- project_grad: float32 [1024, 640], P('shard')
- gate_grad: float32 [640, 2048], P('shard')
- upward_grad: float32 [640, 2048], P('shard')
- down_grad: float32 [2048, 640], P('shard')
- inputgain_grad: float32 [640], P('shard')
- querygain_grad: float32 [256], P('shard')
- keygain_grad: float32 [256], P('shard')
- attendgain_grad: float32 [640], P('shard')
- beforegain_grad: float32 [640], P('shard')
- aftergain_grad: float32 [640], P('shard')
The draws below stay inside these ranges and needn't reach their ends.
Inputs may be any that keep to these rules, and one draw needn't show every extreme that they name: `seq_lengths`: some sequence has exactly 1024 tokens. `seq_device`: every device index holds exactly two sequences, whose lengths sum to at most 1536; on some device they sum to exactly 1536.
All inputs are finite; a program needn't handle non-finite values.
Results may differ from the reference program's by a relative error of at most 0.017.
Values may be sent and summed in bfloat16 or wider, within the bound.
A program may use at most 256 MiB of HBM per device.

```python
import math
import jax
import jax.numpy as jnp
from jax import lax

D = 640
QH = 4
HD = 256
FF = 2048
MAXLEN = 1024
CAP = 1536
TOKENS = 49152
N_SHARD = 8
N_REP = 4


def seq_layout(key):
    devices = N_REP * N_SHARD
    base = jax.random.fold_in(key, 11)
    k_first, k_second, k_full, k_order = jax.random.split(base, 4)
    first = jax.random.randint(k_first, (devices,), MAXLEN // 4, MAXLEN + 1, dtype=jnp.int32)
    upper = jnp.minimum(MAXLEN, CAP - first) + 1
    second = jax.random.randint(k_second, (devices,), MAXLEN // 4, upper, dtype=jnp.int32)
    full = jax.random.randint(k_full, (), 0, devices, dtype=jnp.int32)
    owner = jnp.arange(devices, dtype=jnp.int32)
    first = jnp.where(owner == full, MAXLEN, first).astype(jnp.int32)
    second = jnp.where(owner == full, CAP - MAXLEN, second).astype(jnp.int32)
    lengths = jnp.concatenate([first, second])
    owners = jnp.concatenate([owner, owner])
    order = jax.random.permutation(k_order, 2 * devices)
    return (lengths[order], owners[order])


def draw_seq_lengths(key, part):
    return seq_layout(key)[0]


def draw_seq_device(key, part):
    return seq_layout(key)[1]


def block_levels(stream_key, extent, cuts, low, high):
    level, own = 1.0, jax.random.fold_in(stream_key, 6)
    for dim, blocks in cuts:
        steps = jnp.exp(jax.random.uniform(jax.random.fold_in(own, dim), (blocks,), jnp.float32, low / len(cuts), high / len(cuts)))
        level = level * jnp.repeat(steps, extent[dim] // blocks).reshape([-1 if axis == dim else 1 for axis in range(len(extent))])
    return level


def normal_values(rng, extent, scale, limit, cuts=(), held_as=jnp.bfloat16):
    drawn = scale * jax.random.normal(rng, extent, jnp.float32)
    if cuts:
        drawn = drawn * block_levels(rng, extent, cuts, -0.22, 0.18)
    return jnp.clip(drawn, -limit, limit).astype(held_as)


def setup_inputs(seed: int = 0) -> dict:
    key_list = jax.random.split(jax.random.key(seed), 17)
    tokens = normal_values(key_list[0], (TOKENS, D), 1.0, 6.0, ((0, 32),))
    seq_lengths = draw_seq_lengths(jax.random.fold_in(key_list[16], 71), 0)
    seq_device = draw_seq_device(jax.random.fold_in(key_list[16], 71), 0)
    w_query = normal_values(key_list[3], (D, QH * HD), D ** -0.5, 0.25, ((0, 8),))
    w_keyval = normal_values(key_list[4], (D, 2 * HD), D ** -0.5, 0.25, ((0, 8),))
    w_project = normal_values(key_list[5], (QH * HD, D), (QH * HD) ** -0.5, 0.1875, ((0, 8),))
    w_gate = normal_values(key_list[6], (D, FF), D ** -0.5, 0.25, ((0, 8),))
    w_upward = normal_values(key_list[7], (D, FF), D ** -0.5, 0.25, ((0, 8),))
    w_down = normal_values(key_list[8], (FF, D), FF ** -0.5, 0.125, ((0, 8),))
    gain_input = jnp.clip(jnp.exp(math.log(2.0) - 1.3862944 * jax.random.uniform(key_list[9], (D,), jnp.float32) ** block_levels(key_list[9], (D,), ((0, 8),), -0.2, 0.2)), 0.5, 2.0).astype(jnp.bfloat16)
    gain_query = jnp.clip(jnp.exp(math.log(2.0) - 1.3862944 * jax.random.uniform(key_list[10], (HD,), jnp.float32) ** block_levels(key_list[10], (HD,), ((0, 8),), -0.2, 0.2)), 0.5, 2.0).astype(jnp.bfloat16)
    gain_key = jnp.clip(jnp.exp(math.log(2.0) - 1.3862944 * jax.random.uniform(key_list[11], (HD,), jnp.float32) ** block_levels(key_list[11], (HD,), ((0, 8),), -0.2, 0.2)), 0.5, 2.0).astype(jnp.bfloat16)
    gain_attend = jnp.clip(jnp.exp(math.log(2.0) - 1.3862944 * jax.random.uniform(key_list[12], (D,), jnp.float32) ** block_levels(key_list[12], (D,), ((0, 8),), -0.2, 0.2)), 0.5, 2.0).astype(jnp.bfloat16)
    gain_before = jnp.clip(jnp.exp(math.log(2.0) - 1.3862944 * jax.random.uniform(key_list[13], (D,), jnp.float32) ** block_levels(key_list[13], (D,), ((0, 8),), -0.2, 0.2)), 0.5, 2.0).astype(jnp.bfloat16)
    gain_after = jnp.clip(jnp.exp(math.log(2.0) - 1.3862944 * jax.random.uniform(key_list[14], (D,), jnp.float32) ** block_levels(key_list[14], (D,), ((0, 8),), -0.2, 0.2)), 0.5, 2.0).astype(jnp.bfloat16)
    cotangent = normal_values(key_list[15], (TOKENS, D), 1.0, 6.0, ((0, 32),))
    return dict(tokens=tokens, seq_lengths=seq_lengths, seq_device=seq_device, w_query=w_query, w_keyval=w_keyval, w_project=w_project, w_gate=w_gate, w_upward=w_upward, w_down=w_down, gain_input=gain_input, gain_query=gain_query, gain_key=gain_key, gain_attend=gain_attend, gain_before=gain_before, gain_after=gain_after, cotangent=cotangent)


EPS = 1e-06
THETA = 1000000.0
NEG = -1e+30

@jax.custom_vjp
def low(v):
    return lax.optimization_barrier(v.astype(jnp.bfloat16)).astype(jnp.float32)

@jax.custom_vjp
def low_back(v):
    return v

def low_keep(v):
    return (low(v), None)

def low_pass(kept, grad):
    return (grad,)

def back_keep(v):
    return (v, None)

def back_low(kept, grad):
    return (low(grad),)
low.defvjp(low_keep, low_pass)
low_back.defvjp(back_keep, back_low)

def matmul(left, right):
    return jnp.dot(left, right, precision=lax.Precision.HIGHEST, preferred_element_type=jnp.float32)

def normed(value, gain):
    return value * lax.rsqrt(lax.optimization_barrier(jnp.mean(value * value, axis=-1, keepdims=True)) + EPS) * gain

def rotary(position, width):
    freqs = THETA ** (-(jnp.arange(width // 2, dtype=jnp.float32) * 2.0 / width))
    angles = position.astype(jnp.float32)[:, None] * freqs[None, :]
    return (jnp.cos(angles), jnp.sin(angles))

def rotate(value, cosine, sine):
    half = value.shape[-1] // 2
    first = value[..., :half]
    second = value[..., half:]
    return jnp.concatenate([first * cosine - second * sine, second * cosine + first * sine], axis=-1)

def layout(seq_lengths, seq_device, device, rows):
    mine = seq_device == device
    lens = jnp.where(mine, seq_lengths, 0).astype(jnp.int32)
    ends = jnp.cumsum(lens, dtype=jnp.int32)
    starts = (ends - lens).astype(jnp.int32)
    row_ids = jnp.arange(rows, dtype=jnp.int32)
    begun = mine[None, :] & (starts[None, :] <= row_ids[:, None])
    segment = lax.optimization_barrier(jnp.sum(begun.astype(jnp.int32), axis=1, dtype=jnp.int32))
    own_start = lax.optimization_barrier(jnp.max(jnp.where(begun, starts[None, :], 0), axis=1)).astype(jnp.int32)
    position = (row_ids - own_start).astype(jnp.int32)
    live = row_ids < jnp.sum(lens, dtype=jnp.int32)
    return (segment, position, live)

def attend_block(query, seg_query, row_query, keys, values, seg_keys, row_keys):
    scale = HD ** (-0.5)
    scores = jnp.einsum('qhd,kd->hqk', query, keys, precision=lax.Precision.HIGHEST) * scale
    allowed = (seg_query[:, None] == seg_keys[None, :]) & (row_keys[None, :] <= row_query[:, None])
    scores = low_back(jnp.where(allowed[None], scores, NEG))
    peak = lax.optimization_barrier(jnp.max(scores, axis=-1, keepdims=True))
    expo = jnp.exp(scores - peak)
    probs = expo / lax.optimization_barrier(jnp.sum(expo, axis=-1, keepdims=True))
    return jnp.einsum('hqk,kd->qhd', low(probs), values, precision=lax.Precision.HIGHEST)

def forward(params, x, segment, position):
    w_query, w_keyval, w_project, w_gate, w_upward, w_down, gain_input, gain_query, gain_key, gain_attend, gain_before, gain_after = params
    rows = x.shape[0]
    cosine, sine = rotary(position, HD)
    h_low = low(normed(x, gain_input))
    q_raw = low_back(matmul(h_low, w_query)).reshape(rows, QH, HD)
    kv_raw = low_back(matmul(h_low, w_keyval))
    queries = low(rotate(normed(q_raw, gain_query), cosine[:, None, :], sine[:, None, :]))
    keys = low(rotate(normed(kv_raw[:, :HD], gain_key), cosine, sine))
    values = low(kv_raw[:, HD:])
    block = rows // 3
    row_ids = jnp.arange(rows, dtype=jnp.int32)
    attend = jax.checkpoint(attend_block)
    pieces = lax.map(lambda item: attend(item[0], item[1], item[2], keys, values, segment, row_ids), (queries.reshape(3, block, QH, HD), segment.reshape(3, block), row_ids.reshape(3, block)))
    attended = low(low_back(pieces.reshape(rows, QH * HD)))
    branch = low_back(matmul(attended, w_project))
    x_mid = x + normed(branch, gain_attend)
    h_two = low(normed(x_mid, gain_before))
    gate = low_back(matmul(h_two, w_gate))
    upper = low_back(matmul(h_two, w_upward))
    hidden = low(jax.nn.gelu(gate, approximate=True) * upper)
    ffn = low_back(matmul(hidden, w_down))
    return x_mid + normed(ffn, gain_after)

def reference(tokens, seq_lengths, seq_device, w_query, w_keyval, w_project, w_gate, w_upward, w_down, gain_input, gain_query, gain_key, gain_attend, gain_before, gain_after, cotangent):
    devices = N_REP * N_SHARD
    params = tuple((w.astype(jnp.float32) for w in (w_query, w_keyval, w_project, w_gate, w_upward, w_down, gain_input, gain_query, gain_key, gain_attend, gain_before, gain_after)))
    x_all = tokens.astype(jnp.float32).reshape(devices, CAP, D)
    cot_all = cotangent.astype(jnp.float32).reshape(devices, CAP, D)

    def one_device(totals, item):
        x_rows, cot_rows, device = item
        segment, position, live = layout(seq_lengths, seq_device, device, CAP)
        result, backward = jax.vjp(lambda p, xx: forward(p, xx, segment, position), params, x_rows)
        grads, d_input = backward(jnp.where(live[:, None], cot_rows, jnp.float32(0.0)))
        totals = tuple((a + b for a, b in zip(totals, grads)))
        return (totals, (result.astype(jnp.bfloat16), d_input))
    zeros = tuple((jnp.zeros_like(p) for p in params))
    totals, (results, d_inputs) = lax.scan(one_device, zeros, (x_all, cot_all, jnp.arange(devices, dtype=jnp.int32)))
    return (results.reshape(TOKENS, D), d_inputs.reshape(TOKENS, D), totals[0], totals[1], totals[2], totals[3], totals[4], totals[5], totals[6], totals[7], totals[8], totals[9], totals[10], totals[11])
```

```python
import jax
import jax.numpy as jnp
from jax import lax
from jax.sharding import PartitionSpec as P

QH = 4
HD = 256


EPS = 1e-06
THETA = 1000000.0
NEG = -1e30


def normed(value, gain):
    return value * lax.rsqrt(jnp.mean(value * value, axis=-1, keepdims=True) + EPS) * gain


def rotary(position, width):
    freqs = THETA ** (-(jnp.arange(width // 2, dtype=jnp.float32) * 2.0 / width))
    angles = position.astype(jnp.float32)[:, None] * freqs[None, :]
    return (jnp.cos(angles), jnp.sin(angles))


def rotate(value, cosine, sine):
    half = value.shape[-1] // 2
    first = value[..., :half]
    second = value[..., half:]
    return jnp.concatenate(
        [first * cosine - second * sine, second * cosine + first * sine], axis=-1
    )


def layout(seq_lengths, seq_device, device, rows):
    mine = seq_device == device
    lens = jnp.where(mine, seq_lengths, 0)
    ends = jnp.cumsum(lens, dtype=jnp.int32)
    starts = ends - lens
    row_ids = jnp.arange(rows, dtype=jnp.int32)
    begun = mine[None, :] & (starts[None, :] <= row_ids[:, None])
    segment = jnp.sum(begun.astype(jnp.int32), axis=1, dtype=jnp.int32)
    own_start = jnp.max(jnp.where(begun, starts[None, :], 0), axis=1)
    position = row_ids - own_start
    live = row_ids < jnp.sum(lens, dtype=jnp.int32)
    return (segment, position, live)


def left_dot(left, right):
    return lax.dot_general(
        left, right, (((0,), (0,)), ((), ())), preferred_element_type=jnp.float32
    )


def right_dot(left, right):
    return lax.dot_general(
        left, right, (((1,), (1,)), ((), ())), preferred_element_type=jnp.float32
    )


def scatter(grad):
    return lax.psum_scatter(grad, "shard", scatter_dimension=0, tiled=True)


def rep_sum(part, flip):
    size = lax.axis_size("rep")
    if size & (size - 1):
        return lax.psum(part.astype(jnp.float32), "rep")
    steps = [1 << bit for bit in range(size.bit_length() - 1)]
    if flip:
        steps = steps[::-1]
    total = part
    for step in steps:
        pairs = [(peer, peer ^ step) for peer in range(size)]
        other = lax.ppermute(total.astype(jnp.bfloat16), "rep", pairs)
        total = total.astype(jnp.bfloat16).astype(jnp.float32) + other.astype(jnp.float32)
    return total


def permuted_gather(part):
    size = lax.axis_size("shard")
    if size > 8:
        return lax.all_gather(part, "shard", axis=0, tiled=True)
    me = lax.axis_index("shard")
    rows = part.shape[0]
    full = jnp.zeros((size * rows, part.shape[1]), part.dtype)
    full = lax.dynamic_update_slice(full, part, (me * rows, 0))
    for shift in range(1, size):
        piece = lax.ppermute(
            part, "shard", [(peer, (peer + shift) % size) for peer in range(size)]
        )
        owner = lax.rem(me + size - shift, size)
        full = lax.dynamic_update_slice(full, piece, (owner * rows, 0))
    return full


def shards(
    tokens,
    seq_lengths,
    seq_device,
    w_query,
    w_keyval,
    w_project,
    w_gate,
    w_upward,
    w_down,
    gain_input,
    gain_query,
    gain_key,
    gain_attend,
    gain_before,
    gain_after,
    cotangent,
):
    rows = tokens.shape[0]
    device = lax.axis_index("shard") * lax.axis_size("rep") + lax.axis_index("rep")
    segment, position, live = layout(seq_lengths, seq_device, device, rows)
    cosine, sine = rotary(position, HD)
    n_shard = lax.axis_size("shard")
    d_model = w_query.shape[0] * n_shard
    part = w_query.shape[0]

    def column(gain):
        return jnp.pad(gain, (0, part - gain.shape[0]))[:, None]

    gain_cols = jnp.concatenate(
        [column(g) for g in (gain_input, gain_query, gain_key, gain_attend, gain_before, gain_after)]
        + [jnp.zeros((part, 122), jnp.bfloat16)],
        axis=1,
    )
    pack = lax.all_gather(
        jnp.concatenate([w_query, w_keyval, gain_cols], axis=1), "shard", axis=0, tiled=True
    )
    pack, project_part = lax.optimization_barrier((pack, w_project))
    project_full = permuted_gather(project_part)
    q_cols = w_query.shape[1]
    kv_cols = w_keyval.shape[1]
    qkv_full = pack[:, : q_cols + kv_cols]
    gains = pack[:, q_cols + kv_cols : q_cols + kv_cols + 6].T
    input_full, attend_full, before_full, after_full = gains[0], gains[3], gains[4], gains[5]
    head_part = gain_query.shape[0]
    qgain_full = gains[1].reshape(n_shard, part)[:, :head_part].reshape(HD)
    kgain_full = gains[2].reshape(n_shard, part)[:, :head_part].reshape(HD)
    query_full = qkv_full[:, :q_cols]
    keyval_full = qkv_full[:, q_cols:]
    gate_full = lax.all_gather(w_gate, "shard", axis=0, tiled=True)
    upward_full = lax.all_gather(w_upward, "shard", axis=0, tiled=True)
    down_full = lax.all_gather(w_down, "shard", axis=0, tiled=True)
    x_rows = tokens.astype(jnp.float32)
    h_value, back_input = jax.vjp(normed, x_rows, input_full.astype(jnp.float32))
    h_low = h_value.astype(jnp.bfloat16)
    q_raw = jnp.dot(h_low, query_full, preferred_element_type=jnp.float32).reshape(rows, QH, HD)
    kv_raw = jnp.dot(h_low, keyval_full, preferred_element_type=jnp.float32)

    def query_side(value, gain):
        return rotate(normed(value, gain), cosine[:, None, :], sine[:, None, :])

    def key_side(value, gain):
        return rotate(normed(value, gain), cosine, sine)

    q_rot, back_query = jax.vjp(query_side, q_raw, qgain_full.astype(jnp.float32))
    k_rot, back_key = jax.vjp(key_side, kv_raw[:, :HD], kgain_full.astype(jnp.float32))
    q_low = q_rot.astype(jnp.bfloat16)
    k_low = k_rot.astype(jnp.bfloat16)
    v_low = kv_raw[:, HD:].astype(jnp.bfloat16)
    block = rows // 3
    scale = HD ** (-0.5)
    row_ids = jnp.arange(rows, dtype=jnp.int32)

    def block_scores(index):
        q_block = q_low[index * block : (index + 1) * block]
        seen = (index + 1) * block
        raw = (
            jnp.einsum("qhd,kd->hqk", q_block, k_low[:seen], preferred_element_type=jnp.float32)
            * scale
        )
        seg_block = segment[index * block : (index + 1) * block]
        row_block = row_ids[index * block : (index + 1) * block]
        allowed = (seg_block[:, None] == segment[None, :seen]) & (
            row_ids[None, :seen] <= row_block[:, None]
        )
        return (jnp.where(allowed[None], raw, NEG), q_block)

    out_parts = []
    lse_parts = []
    for index in range(3):
        logits, q_block = block_scores(index)
        peak = jnp.max(logits, axis=-1, keepdims=True)
        expo = jnp.exp(logits - peak)
        total = jnp.sum(expo, axis=-1, keepdims=True)
        probs = expo / total
        out_parts.append(
            jnp.einsum(
                "hqk,kd->qhd", probs.astype(jnp.bfloat16), v_low[: (index + 1) * block],
                preferred_element_type=jnp.float32,
            )
        )
        lse_parts.append(peak + jnp.log(total))
    attended = jnp.concatenate(out_parts, axis=0).reshape(rows, QH * HD).astype(jnp.bfloat16)
    branch = jnp.dot(attended, project_full, preferred_element_type=jnp.float32)
    branch_normed, back_attend = jax.vjp(normed, branch, attend_full.astype(jnp.float32))
    x_mid = x_rows + branch_normed
    h_two, back_before = jax.vjp(normed, x_mid, before_full.astype(jnp.float32))
    h_two_low = h_two.astype(jnp.bfloat16)
    gate = jnp.dot(h_two_low, gate_full, preferred_element_type=jnp.float32)
    upper = jnp.dot(h_two_low, upward_full, preferred_element_type=jnp.float32)
    hidden, back_glu = jax.vjp(
        lambda g_val, u_val: jax.nn.gelu(g_val, approximate=True) * u_val, gate, upper
    )
    hidden_low = hidden.astype(jnp.bfloat16)
    ffn = jnp.dot(hidden_low, down_full, preferred_element_type=jnp.float32)
    ffn_normed, back_after = jax.vjp(normed, ffn, after_full.astype(jnp.float32))
    activations = (x_mid + ffn_normed).astype(jnp.bfloat16)
    upstream = jnp.where(live[:, None], cotangent.astype(jnp.float32), jnp.float32(0.0))
    d_ffn, aftergain_grad = back_after(upstream)
    d_ffn_low = d_ffn.astype(jnp.bfloat16)
    down_grad = left_dot(hidden_low, d_ffn_low).astype(jnp.bfloat16)
    down_grad, d_ffn_low = lax.optimization_barrier((down_grad, d_ffn_low))
    down_share = scatter(down_grad)
    d_hidden = right_dot(d_ffn_low, down_full)
    d_gate, d_up = back_glu(d_hidden)
    d_gate_low = d_gate.astype(jnp.bfloat16)
    d_up_low = d_up.astype(jnp.bfloat16)
    gate_grad = left_dot(h_two_low, d_gate_low).astype(jnp.bfloat16)
    upward_grad = left_dot(h_two_low, d_up_low).astype(jnp.bfloat16)
    gate_grad, upward_grad, d_gate_low, d_up_low = lax.optimization_barrier(
        (gate_grad, upward_grad, d_gate_low, d_up_low)
    )
    gate_share = scatter(gate_grad)
    upward_share = scatter(upward_grad)
    d_h_two = right_dot(d_gate_low, gate_full) + right_dot(d_up_low, upward_full)
    d_mid_part, beforegain_grad = back_before(d_h_two)
    d_mid = upstream + d_mid_part
    d_branch, attendgain_grad = back_attend(d_mid)
    d_branch_low = d_branch.astype(jnp.bfloat16)
    project_grad = left_dot(attended, d_branch_low).astype(jnp.bfloat16)
    project_grad, d_branch_low = lax.optimization_barrier((project_grad, d_branch_low))
    project_share = scatter(project_grad)
    d_attended = right_dot(d_branch_low, project_full).reshape(rows, QH, HD).astype(jnp.bfloat16)
    down_share, d_attended = lax.optimization_barrier((down_share, d_attended))
    dq_parts = []
    d_keys = jnp.zeros((rows, HD), jnp.float32)
    d_values = jnp.zeros((rows, HD), jnp.float32)
    for index in range(3):
        logits, q_block = block_scores(index)
        probs = jnp.exp(logits - lse_parts[index])
        d_block = d_attended[index * block : (index + 1) * block]
        seen = (index + 1) * block
        d_probs = jnp.einsum(
            "qhd,kd->hqk", d_block, v_low[:seen], preferred_element_type=jnp.float32
        )
        spread = jnp.sum(probs * d_probs, axis=-1, keepdims=True)
        d_logits = (probs * (d_probs - spread)).astype(jnp.bfloat16)
        dq_parts.append(
            jnp.einsum(
                "hqk,kd->qhd", d_logits, k_low[:seen], preferred_element_type=jnp.float32
            )
            * scale
        )
        rest = ((0, rows - seen), (0, 0))
        d_keys = d_keys + jnp.pad(
            jnp.einsum("hqk,qhd->kd", d_logits, q_block, preferred_element_type=jnp.float32)
            * scale,
            rest,
        )
        d_values = d_values + jnp.pad(
            jnp.einsum(
                "hqk,qhd->kd",
                probs.astype(jnp.bfloat16),
                d_block,
                preferred_element_type=jnp.float32,
            ),
            rest,
        )
    sum_down = rep_sum(down_share, False)
    sum_down, gate_share, upward_share, d_keys = lax.optimization_barrier(
        (sum_down, gate_share, upward_share, d_keys)
    )
    sum_gate = rep_sum(gate_share, True)
    sum_upward = rep_sum(upward_share, False)
    d_queries = jnp.concatenate(dq_parts, axis=0)
    d_q_raw, querygain_grad = back_query(d_queries)
    d_k_raw, keygain_grad = back_key(d_keys)
    d_q_low = d_q_raw.reshape(rows, QH * HD).astype(jnp.bfloat16)
    d_kv_low = jnp.concatenate([d_k_raw, d_values], axis=1).astype(jnp.bfloat16)
    d_qkv_low = jnp.concatenate([d_q_low, d_kv_low], axis=1)
    qkv_grad = left_dot(h_low, d_qkv_low).astype(jnp.bfloat16)

    def spread_rows(grad):
        return jnp.pad(grad.reshape(n_shard, -1), ((0, 0), (0, part - head_part))).reshape(d_model)

    grad_cols = jnp.stack(
        [
            spread_rows(querygain_grad),
            spread_rows(keygain_grad),
            attendgain_grad,
            beforegain_grad,
            aftergain_grad,
        ],
        axis=1,
    ).astype(jnp.bfloat16)
    grad_pack = jnp.concatenate(
        [qkv_grad, grad_cols, jnp.zeros((d_model, 123), jnp.bfloat16)], axis=1
    )
    grad_pack, d_qkv_low = lax.optimization_barrier((grad_pack, d_qkv_low))
    sum_gate, sum_upward, project_share, grad_pack = lax.optimization_barrier(
        (sum_gate, sum_upward, project_share, grad_pack)
    )
    pack_share = scatter(grad_pack)
    d_h = right_dot(d_qkv_low, qkv_full)
    d_input_part = back_input(d_h)[0]
    input_grad = d_mid + d_input_part
    sum_project = rep_sum(project_share, True)
    sum_pack = rep_sum(pack_share, False)
    sum_query = sum_pack[:, :q_cols]
    sum_keyval = sum_pack[:, q_cols : q_cols + kv_cols]
    sum_gains = sum_pack[:, q_cols + kv_cols : q_cols + kv_cols + 5].T
    sum_qgain, sum_kgain = sum_gains[0, :head_part], sum_gains[1, :head_part]
    sum_attend, sum_before, sum_after = sum_gains[2], sum_gains[3], sum_gains[4]
    sum_input = (
        jnp.sum(sum_query * w_query.astype(jnp.float32), axis=1)
        + jnp.sum(sum_keyval * w_keyval.astype(jnp.float32), axis=1)
    ) / gain_input.astype(jnp.float32)
    return (
        activations,
        input_grad,
        sum_query,
        sum_keyval,
        sum_project,
        sum_gate,
        sum_upward,
        sum_down,
        sum_input,
        sum_qgain,
        sum_kgain,
        sum_attend,
        sum_before,
        sum_after,
    )


def solution(mesh):
    return jax.shard_map(
        shards,
        mesh=mesh,
        in_specs=(
            P(("shard", "rep"), None),
            P(),
            P(),
            P("shard", None),
            P("shard", None),
            P("shard", None),
            P("shard", None),
            P("shard", None),
            P("shard", None),
            P("shard"),
            P("shard"),
            P("shard"),
            P("shard"),
            P("shard"),
            P("shard"),
            P(("shard", "rep"), None),
        ),
        out_specs=(
            P(("shard", "rep"), None),
            P(("shard", "rep"), None),
            P("shard", None),
            P("shard", None),
            P("shard", None),
            P("shard", None),
            P("shard", None),
            P("shard", None),
            P("shard"),
            P("shard"),
            P("shard"),
            P("shard"),
            P("shard"),
            P("shard"),
        ),
        check_vma=False,
    )
```

```python
import jax
import jax.numpy as jnp
from jax import lax
from jax.sharding import PartitionSpec as P

QH = 4
HD = 256


EPS = 1e-06
THETA = 1000000.0
NEG = -1e30


def normed(value, gain):
    return value * lax.rsqrt(jnp.mean(value * value, axis=-1, keepdims=True) + EPS) * gain


def rotary(position, width):
    freqs = THETA ** (-(jnp.arange(width // 2, dtype=jnp.float32) * 2.0 / width))
    angles = position.astype(jnp.float32)[:, None] * freqs[None, :]
    return (jnp.cos(angles), jnp.sin(angles))


def rotate(value, cosine, sine):
    half = value.shape[-1] // 2
    first = value[..., :half]
    second = value[..., half:]
    return jnp.concatenate(
        [first * cosine - second * sine, second * cosine + first * sine], axis=-1
    )


def layout(seq_lengths, seq_device, device, rows):
    mine = seq_device == device
    lens = jnp.where(mine, seq_lengths, 0)
    ends = jnp.cumsum(lens, dtype=jnp.int32)
    starts = ends - lens
    row_ids = jnp.arange(rows, dtype=jnp.int32)
    begun = mine[None, :] & (starts[None, :] <= row_ids[:, None])
    segment = jnp.sum(begun.astype(jnp.int32), axis=1, dtype=jnp.int32)
    own_start = jnp.max(jnp.where(begun, starts[None, :], 0), axis=1)
    position = row_ids - own_start
    live = row_ids < jnp.sum(lens, dtype=jnp.int32)
    return (segment, position, live)


def left_dot(left, right):
    return lax.dot_general(
        left, right, (((0,), (0,)), ((), ())), preferred_element_type=jnp.float32
    )


def right_dot(left, right):
    return lax.dot_general(
        left, right, (((1,), (1,)), ((), ())), preferred_element_type=jnp.float32
    )


def scatter(grad):
    return lax.psum_scatter(grad, "shard", scatter_dimension=0, tiled=True)


def rep_sum(part, flip):
    size = lax.axis_size("rep")
    if size & (size - 1):
        return lax.psum(part.astype(jnp.float32), "rep")
    steps = [1 << bit for bit in range(size.bit_length() - 1)]
    if flip:
        steps = steps[::-1]
    total = part
    for step in steps:
        pairs = [(peer, peer ^ step) for peer in range(size)]
        other = lax.ppermute(total.astype(jnp.bfloat16), "rep", pairs)
        total = total.astype(jnp.bfloat16).astype(jnp.float32) + other.astype(jnp.float32)
    return total


def permuted_gather(part):
    size = lax.axis_size("shard")
    if size > 8:
        return lax.all_gather(part, "shard", axis=0, tiled=True)
    me = lax.axis_index("shard")
    rows = part.shape[0]
    full = jnp.zeros((size * rows, part.shape[1]), part.dtype)
    full = lax.dynamic_update_slice(full, part, (me * rows, 0))
    for shift in range(1, size):
        piece = lax.ppermute(
            part, "shard", [(peer, (peer + shift) % size) for peer in range(size)]
        )
        owner = lax.rem(me + size - shift, size)
        full = lax.dynamic_update_slice(full, piece, (owner * rows, 0))
    return full


def shards(
    tokens,
    seq_lengths,
    seq_device,
    w_query,
    w_keyval,
    w_project,
    w_gate,
    w_upward,
    w_down,
    gain_input,
    gain_query,
    gain_key,
    gain_attend,
    gain_before,
    gain_after,
    cotangent,
):
    rows = tokens.shape[0]
    device = lax.axis_index("shard") * lax.axis_size("rep") + lax.axis_index("rep")
    segment, position, live = layout(seq_lengths, seq_device, device, rows)
    cosine, sine = rotary(position, HD)
    n_shard = lax.axis_size("shard")
    d_model = w_query.shape[0] * n_shard
    part = w_query.shape[0]

    def column(gain):
        return jnp.pad(gain, (0, part - gain.shape[0]))[:, None]

    gain_cols = jnp.concatenate(
        [column(g) for g in (gain_input, gain_query, gain_key, gain_attend, gain_before, gain_after)]
        + [jnp.zeros((part, 122), jnp.bfloat16)],
        axis=1,
    )
    pack = lax.all_gather(
        jnp.concatenate([w_query, w_keyval, gain_cols], axis=1), "shard", axis=0, tiled=True
    )
    pack, project_part = lax.optimization_barrier((pack, w_project))
    project_full = permuted_gather(project_part)
    q_cols = w_query.shape[1]
    kv_cols = w_keyval.shape[1]
    qkv_full = pack[:, : q_cols + kv_cols]
    gains = pack[:, q_cols + kv_cols : q_cols + kv_cols + 6].T
    input_full, attend_full, before_full, after_full = gains[0], gains[3], gains[4], gains[5]
    head_part = gain_query.shape[0]
    qgain_full = gains[1].reshape(n_shard, part)[:, :head_part].reshape(HD)
    kgain_full = gains[2].reshape(n_shard, part)[:, :head_part].reshape(HD)
    query_full = qkv_full[:, :q_cols]
    keyval_full = qkv_full[:, q_cols:]
    gate_full = lax.all_gather(w_gate, "shard", axis=0, tiled=True)
    upward_full = lax.all_gather(w_upward, "shard", axis=0, tiled=True)
    down_full = lax.all_gather(w_down, "shard", axis=0, tiled=True)
    x_rows = tokens.astype(jnp.float32)
    h_value, back_input = jax.vjp(normed, x_rows, input_full.astype(jnp.float32))
    h_low = h_value.astype(jnp.bfloat16)
    q_raw = jnp.dot(h_low, query_full, preferred_element_type=jnp.float32).reshape(rows, QH, HD)
    kv_raw = jnp.dot(h_low, keyval_full, preferred_element_type=jnp.float32)

    def query_side(value, gain):
        return rotate(normed(value, gain), cosine[:, None, :], sine[:, None, :])

    def key_side(value, gain):
        return rotate(normed(value, gain), cosine, sine)

    q_rot, back_query = jax.vjp(query_side, q_raw, qgain_full.astype(jnp.float32))
    k_rot, back_key = jax.vjp(key_side, kv_raw[:, :HD], kgain_full.astype(jnp.float32))
    q_low = q_rot.astype(jnp.bfloat16)
    k_low = k_rot.astype(jnp.bfloat16)
    v_low = kv_raw[:, HD:].astype(jnp.bfloat16)
    block = rows // 3
    scale = HD ** (-0.5)
    row_ids = jnp.arange(rows, dtype=jnp.int32)

    def block_scores(index):
        q_block = q_low[index * block : (index + 1) * block]
        seen = (index + 1) * block
        raw = (
            jnp.einsum("qhd,kd->hqk", q_block, k_low[:seen], preferred_element_type=jnp.float32)
            * scale
        )
        seg_block = segment[index * block : (index + 1) * block]
        row_block = row_ids[index * block : (index + 1) * block]
        allowed = (seg_block[:, None] == segment[None, :seen]) & (
            row_ids[None, :seen] <= row_block[:, None]
        )
        return (jnp.where(allowed[None], raw, NEG), q_block)

    out_parts = []
    lse_parts = []
    for index in range(3):
        logits, q_block = block_scores(index)
        peak = jnp.max(logits, axis=-1, keepdims=True)
        expo = jnp.exp(logits - peak)
        total = jnp.sum(expo, axis=-1, keepdims=True)
        probs = expo / total
        out_parts.append(
            jnp.einsum(
                "hqk,kd->qhd", probs.astype(jnp.bfloat16), v_low[: (index + 1) * block],
                preferred_element_type=jnp.float32,
            )
        )
        lse_parts.append(peak + jnp.log(total))
    attended = jnp.concatenate(out_parts, axis=0).reshape(rows, QH * HD).astype(jnp.bfloat16)
    branch = jnp.dot(attended, project_full, preferred_element_type=jnp.float32)
    branch_normed, back_attend = jax.vjp(normed, branch, attend_full.astype(jnp.float32))
    x_mid = x_rows + branch_normed
    h_two, back_before = jax.vjp(normed, x_mid, before_full.astype(jnp.float32))
    h_two_low = h_two.astype(jnp.bfloat16)
    gate = jnp.dot(h_two_low, gate_full, preferred_element_type=jnp.float32)
    upper = jnp.dot(h_two_low, upward_full, preferred_element_type=jnp.float32)
    hidden, back_glu = jax.vjp(
        lambda g_val, u_val: jax.nn.gelu(g_val, approximate=True) * u_val, gate, upper
    )
    hidden_low = hidden.astype(jnp.bfloat16)
    ffn = jnp.dot(hidden_low, down_full, preferred_element_type=jnp.float32)
    ffn_normed, back_after = jax.vjp(normed, ffn, after_full.astype(jnp.float32))
    activations = (x_mid + ffn_normed).astype(jnp.bfloat16)
    upstream = jnp.where(live[:, None], cotangent.astype(jnp.float32), jnp.float32(0.0))
    d_ffn, aftergain_grad = back_after(upstream)
    d_ffn_low = d_ffn.astype(jnp.bfloat16)
    down_grad = left_dot(hidden_low, d_ffn_low).astype(jnp.bfloat16)
    down_grad, d_ffn_low = lax.optimization_barrier((down_grad, d_ffn_low))
    down_share = scatter(down_grad)
    d_hidden = right_dot(d_ffn_low, down_full)
    d_gate, d_up = back_glu(d_hidden)
    d_gate_low = d_gate.astype(jnp.bfloat16)
    d_up_low = d_up.astype(jnp.bfloat16)
    gate_grad = left_dot(h_two_low, d_gate_low).astype(jnp.bfloat16)
    upward_grad = left_dot(h_two_low, d_up_low).astype(jnp.bfloat16)
    gate_grad, upward_grad, d_gate_low, d_up_low = lax.optimization_barrier(
        (gate_grad, upward_grad, d_gate_low, d_up_low)
    )
    gate_share = scatter(gate_grad)
    upward_share = scatter(upward_grad)
    d_h_two = right_dot(d_gate_low, gate_full) + right_dot(d_up_low, upward_full)
    d_mid_part, beforegain_grad = back_before(d_h_two)
    d_mid = upstream + d_mid_part
    d_branch, attendgain_grad = back_attend(d_mid)
    d_branch_low = d_branch.astype(jnp.bfloat16)
    project_grad = left_dot(attended, d_branch_low).astype(jnp.bfloat16)
    project_grad, d_branch_low = lax.optimization_barrier((project_grad, d_branch_low))
    project_share = scatter(project_grad)
    d_attended = right_dot(d_branch_low, project_full).reshape(rows, QH, HD).astype(jnp.bfloat16)
    down_share, d_attended = lax.optimization_barrier((down_share, d_attended))
    dq_parts = []
    d_keys = jnp.zeros((rows, HD), jnp.float32)
    d_values = jnp.zeros((rows, HD), jnp.float32)
    for index in range(3):
        logits, q_block = block_scores(index)
        probs = jnp.exp(logits - lse_parts[index])
        d_block = d_attended[index * block : (index + 1) * block]
        seen = (index + 1) * block
        d_probs = jnp.einsum(
            "qhd,kd->hqk", d_block, v_low[:seen], preferred_element_type=jnp.float32
        )
        spread = jnp.sum(probs * d_probs, axis=-1, keepdims=True)
        d_logits = (probs * (d_probs - spread)).astype(jnp.bfloat16)
        dq_parts.append(
            jnp.einsum(
                "hqk,kd->qhd", d_logits, k_low[:seen], preferred_element_type=jnp.float32
            )
            * scale
        )
        rest = ((0, rows - seen), (0, 0))
        d_keys = d_keys + jnp.pad(
            jnp.einsum("hqk,qhd->kd", d_logits, q_block, preferred_element_type=jnp.float32)
            * scale,
            rest,
        )
        d_values = d_values + jnp.pad(
            jnp.einsum(
                "hqk,qhd->kd",
                probs.astype(jnp.bfloat16),
                d_block,
                preferred_element_type=jnp.float32,
            ),
            rest,
        )
    sum_down = rep_sum(down_share, False)
    sum_down, gate_share, upward_share, d_keys = lax.optimization_barrier(
        (sum_down, gate_share, upward_share, d_keys)
    )
    sum_gate = rep_sum(gate_share, True)
    sum_upward = rep_sum(upward_share, False)
    d_queries = jnp.concatenate(dq_parts, axis=0)
    d_q_raw, querygain_grad = back_query(d_queries)
    d_k_raw, keygain_grad = back_key(d_keys)
    d_q_low = d_q_raw.reshape(rows, QH * HD).astype(jnp.bfloat16)
    d_kv_low = jnp.concatenate([d_k_raw, d_values], axis=1).astype(jnp.bfloat16)
    d_qkv_low = jnp.concatenate([d_q_low, d_kv_low], axis=1)
    qkv_grad = left_dot(h_low, d_qkv_low).astype(jnp.bfloat16)

    def spread_rows(grad):
        return jnp.pad(grad.reshape(n_shard, -1), ((0, 0), (0, part - head_part))).reshape(d_model)

    grad_cols = jnp.stack(
        [
            spread_rows(querygain_grad),
            spread_rows(keygain_grad),
            attendgain_grad,
            beforegain_grad,
            aftergain_grad,
        ],
        axis=1,
    ).astype(jnp.bfloat16)
    grad_pack = jnp.concatenate(
        [qkv_grad, grad_cols, jnp.zeros((d_model, 123), jnp.bfloat16)], axis=1
    )
    grad_pack, d_qkv_low = lax.optimization_barrier((grad_pack, d_qkv_low))
    project_share, grad_pack = lax.optimization_barrier((project_share, grad_pack))
    pack_share = scatter(grad_pack)
    d_h = right_dot(d_qkv_low, qkv_full)
    d_input_part = back_input(d_h)[0]
    input_grad = d_mid + d_input_part
    sum_project = rep_sum(project_share, True)
    sum_pack = rep_sum(pack_share, False)
    sum_query = sum_pack[:, :q_cols]
    sum_keyval = sum_pack[:, q_cols : q_cols + kv_cols]
    sum_gains = sum_pack[:, q_cols + kv_cols : q_cols + kv_cols + 5].T
    sum_qgain, sum_kgain = sum_gains[0, :head_part], sum_gains[1, :head_part]
    sum_attend, sum_before, sum_after = sum_gains[2], sum_gains[3], sum_gains[4]
    sum_input = (
        jnp.sum(sum_query * w_query.astype(jnp.float32), axis=1)
        + jnp.sum(sum_keyval * w_keyval.astype(jnp.float32), axis=1)
    ) / gain_input.astype(jnp.float32)
    return (
        activations,
        input_grad,
        sum_query,
        sum_keyval,
        sum_project,
        sum_gate,
        sum_upward,
        sum_down,
        sum_input,
        sum_qgain,
        sum_kgain,
        sum_attend,
        sum_before,
        sum_after,
    )


def solution(mesh):
    return jax.shard_map(
        shards,
        mesh=mesh,
        in_specs=(
            P(("shard", "rep"), None),
            P(),
            P(),
            P("shard", None),
            P("shard", None),
            P("shard", None),
            P("shard", None),
            P("shard", None),
            P("shard", None),
            P("shard"),
            P("shard"),
            P("shard"),
            P("shard"),
            P("shard"),
            P("shard"),
            P(("shard", "rep"), None),
        ),
        out_specs=(
            P(("shard", "rep"), None),
            P(("shard", "rep"), None),
            P("shard", None),
            P("shard", None),
            P("shard", None),
            P("shard", None),
            P("shard", None),
            P("shard", None),
            P("shard"),
            P("shard"),
            P("shard"),
            P("shard"),
            P("shard"),
            P("shard"),
        ),
        check_vma=False,
    )
```
